128 devices in a mesh: tm: 4 (over y), space: 32 (over z, x, core).
Axes of the slice: x: 4, y: 4, z: 4, core: 2. Of those that a mesh axis runs over, the one named last changes fastest.
Arguments:
- frames: bfloat16 [16, 128, 64, 2048], P('tm', 'space'), may hold values from -60 to 60
- spatial_taps: bfloat16 [9, 2048], replicated, may hold values from -2 to 2
- time_taps: bfloat16 [3, 2048], replicated, may hold values from -2.5 to 2.5
- norm_gain: float32 [2048], replicated, may hold values from 0.1 to 1.9
- w_qkv: bfloat16 [2048, 3072], replicated, may hold values from -0.125 to 0.125
- w_out: bfloat16 [1024, 2048], replicated, may hold values from -0.1875 to 0.1875
- out_gain: float32 [2048], replicated, may hold values from 0.1 to 1.9
Outputs:
- attended: bfloat16 [16, 128, 64, 2048], P('tm', 'space')
The draws below stay inside these ranges and needn't reach their ends.
All inputs are finite; a program needn't handle non-finite values.
Results may differ from the reference program's by a relative error of at most 0.0049.
Values may be sent and summed in bfloat16 or wider, within the bound.
No kernel may reach another device: no remote copies, remote signals or barrier semaphores. Data moves between devices by JAX's collectives and lax.ppermute only.
A program may use at most 128 MiB of HBM per device.

```python
import math
import jax
import jax.numpy as jnp
from jax import lax

C = 2048
HEADS = 8
HEAD = 128
ROWS_DEV = 4
WIDE = 64
QK = 1024
FRAMES = 16
HEIGHT = 128


def draw_frames(key, part):
    key_base, key_offset, key_chan, key_tok = jax.random.split(key, 4)
    blocks = HEIGHT // ROWS_DEV
    offset = jax.random.normal(key_offset, (FRAMES, blocks, 1, 1, C), jnp.float32)
    chan_scale = jnp.exp(jax.random.uniform(key_chan, (C,), jnp.float32, math.log(0.3), math.log(3.0)))
    tok_scale = jnp.exp(jax.random.uniform(key_tok, (FRAMES, HEIGHT, WIDE, 1), jnp.float32, math.log(0.3), math.log(3.0)))
    base = jax.random.normal(key_base, (FRAMES, blocks, ROWS_DEV, WIDE, C), jnp.float32)
    field = (base + offset).reshape(FRAMES, HEIGHT, WIDE, C) * chan_scale * tok_scale
    return jnp.clip(field, -60.0, 60.0).astype(jnp.bfloat16)


def bell_draw(stream_key, dims, width, most, kind=jnp.bfloat16):
    values = jax.random.normal(stream_key, dims, jnp.float32) * width
    return jnp.minimum(jnp.maximum(values, -most), most).astype(kind)


def setup_inputs(seed: int = 0) -> dict:
    arg_keys = jax.random.split(jax.random.key(seed), 8)
    return {
        "frames": draw_frames(jax.random.fold_in(arg_keys[7], 71), 0),
        "spatial_taps": bell_draw(arg_keys[1], (9, C), 0.33, 2.0),
        "time_taps": bell_draw(arg_keys[2], (3, C), 0.5, 2.5),
        "norm_gain": jnp.clip(1.0 + 0.18 * jax.random.normal(arg_keys[3], (C,), jnp.float32), 0.1, 1.9),
        "w_qkv": bell_draw(arg_keys[4], (C, 3 * QK), C ** -0.5, 0.125),
        "w_out": bell_draw(arg_keys[5], (QK, C), QK ** -0.5, 0.1875),
        "out_gain": jnp.clip(1.0 + 0.18 * jax.random.normal(arg_keys[6], (C,), jnp.float32), 0.1, 1.9),
    }


epsilon = 1e-06

def feature_map(inputs):
    return jax.nn.elu(inputs) + 1.0

def reference(frames, spatial_taps, time_taps, norm_gain, w_qkv, w_out, out_gain):
    frame_count, height_rows, col_count, channels = frames.shape
    width_qk = HEADS * HEAD
    tap_weights = spatial_taps.astype(jnp.float32)
    time_weights = time_taps.astype(jnp.float32)
    highest = lax.Precision.HIGHEST

    def spatial(frame_now):
        padded = jnp.pad(frame_now.astype(jnp.float32), ((1, 1), (1, 1), (0, 0)))
        filtered = jnp.zeros((height_rows, col_count, channels), jnp.float32)
        for row_off in range(3):
            for col_off in range(3):
                filtered = filtered + tap_weights[3 * row_off + col_off] * padded[row_off:row_off + height_rows, col_off:col_off + col_count, :]
        return filtered.astype(jnp.bfloat16)

    def advance(carried, frame_now):
        prev_one, prev_two, state_kv, state_z = carried
        smooth = spatial(frame_now)
        mixed_time = time_weights[0] * smooth.astype(jnp.float32) + time_weights[1] * prev_one.astype(jnp.float32) + time_weights[2] * prev_two.astype(jnp.float32)
        hidden = frame_now.astype(jnp.float32) + mixed_time
        flat_tokens = hidden.reshape(height_rows * col_count, channels)
        inverse_rms = lax.rsqrt(lax.optimization_barrier(jnp.mean(flat_tokens * flat_tokens, axis=1, keepdims=True)) + epsilon)
        normed = (flat_tokens * inverse_rms * norm_gain).astype(jnp.bfloat16)
        projected = jnp.dot(normed, w_qkv, preferred_element_type=jnp.float32)
        queries = feature_map(projected[:, :width_qk]).astype(jnp.bfloat16)
        keys_mapped = feature_map(projected[:, width_qk:2 * width_qk]).astype(jnp.bfloat16)
        values_kept = projected[:, 2 * width_qk:].astype(jnp.bfloat16)
        query_heads = queries.astype(jnp.float32).reshape(-1, HEADS, HEAD)
        key_heads = keys_mapped.astype(jnp.float32).reshape(-1, HEADS, HEAD)
        value_heads = values_kept.astype(jnp.float32).reshape(-1, HEADS, HEAD)
        state_kv = state_kv + jnp.einsum('thd,the->hde', key_heads, value_heads, precision=highest)
        state_z = state_z + lax.optimization_barrier(jnp.sum(key_heads, axis=0))
        numerator = jnp.einsum('thd,hde->the', query_heads, state_kv, precision=highest)
        denominator = jnp.einsum('thd,hd->th', query_heads, state_z, precision=highest)
        mixed_heads = (numerator / denominator[:, :, None]).astype(jnp.bfloat16).reshape(-1, width_qk)
        branch = jnp.dot(mixed_heads, w_out, preferred_element_type=jnp.float32)
        out_rms = lax.rsqrt(lax.optimization_barrier(jnp.mean(branch * branch, axis=1, keepdims=True)) + epsilon)
        result = (branch * out_rms * out_gain).astype(jnp.bfloat16).reshape(height_rows, col_count, channels)
        return ((smooth, prev_one, state_kv, state_z), result)
    start_frame = jnp.zeros((height_rows, col_count, channels), jnp.bfloat16)
    initial = (start_frame, start_frame, jnp.zeros((HEADS, HEAD, HEAD), jnp.float32), jnp.zeros((HEADS, HEAD), jnp.float32))
    final_carry, outputs = lax.scan(advance, initial, frames)
    return outputs
```

```python
import functools

import jax
import jax.numpy as jnp
from jax import lax
from jax.experimental import pallas as pl
from jax.experimental.pallas import tpu as pltpu
from jax.sharding import PartitionSpec as P

HEADS = 8
HEAD = 128
C = 2048
WIDE = 64
ROWS = 4
ST = 144
F32 = jnp.float32
BF16 = jnp.bfloat16
epsilon = 1e-06


def space_pairs(move):
    pairs = []
    for s in range(32):
        z, x, c = s // 8, (s // 2) % 4, s % 2
        z2, x2, c2 = move(z, x, c)
        pairs.append((s, (z2 * 4 + x2) * 2 + c2))
    return pairs


def along_core(a):
    return lax.ppermute(a, "space", space_pairs(lambda z, x, c: (z, x, 1 - c)))


def along_x(a, r):
    return lax.ppermute(a, "space", space_pairs(lambda z, x, c: (z, x ^ r, c)))


def along_z(a, r):
    return lax.ppermute(a, "space", space_pairs(lambda z, x, c: (z ^ r, x, c)))


def along_tm(a, by):
    return lax.ppermute(a, "tm", [(i, i + by) for i in range(4 - by)])


def conv_kernel(rows, halo, x_ref, *refs):
    if halo:
        up_ref, down_ref, taps_ref, out_ref = refs
    else:
        taps_ref, out_ref = refs
    lanes = x_ref.shape[-1]

    def body(k, carry):
        ds = pl.ds(pl.multiple_of(k * 128, 128), 128)
        taps = taps_ref[:, ds].astype(F32)
        w = [taps[i : i + 1] for i in range(9)]
        place = lax.broadcasted_iota(jnp.int32, (WIDE, 128), 0)
        first, last = place == 0, place == WIDE - 1
        for f in range(2):
            held = {}

            def get(i):
                if i not in held:
                    if i < 0:
                        held[i] = up_ref[f, 0, :, ds].astype(F32)
                    elif i >= ROWS:
                        held[i] = down_ref[f, 0, :, ds].astype(F32)
                    else:
                        held[i] = x_ref[f, i, :, ds].astype(F32)
                return held[i]

            for n, i in enumerate(rows):
                a, m, b = get(i - 1), get(i), get(i + 1)
                left = w[0] * a + w[3] * m + w[6] * b
                mid = w[1] * a + w[4] * m + w[7] * b
                right = w[2] * a + w[5] * m + w[8] * b
                left = jnp.where(first, 0.0, pltpu.roll(left, 1, 0))
                right = jnp.where(last, 0.0, pltpu.roll(right, WIDE - 1, 0))
                out_ref[f, n, :, ds] = (left + mid + right).astype(BF16)
        return carry

    lax.fori_loop(0, lanes // 128, body, 0)


def conv(frames, pair, rows, halo, taps, name):
    cb = 512
    ins = [frames]
    specs = [pl.BlockSpec((2, ROWS, WIDE, cb), lambda j: (pair, 0, 0, j))]
    if halo is not None:
        ins += list(halo)
        specs += [pl.BlockSpec((2, 1, WIDE, cb), lambda j: (0, 0, 0, j))] * 2
    ins.append(taps)
    specs.append(pl.BlockSpec((9, cb), lambda j: (0, j)))
    n = len(rows)
    return pl.pallas_call(
        functools.partial(conv_kernel, rows, halo is not None),
        grid=(C // cb,),
        in_specs=specs,
        out_specs=pl.BlockSpec((2, n, WIDE, cb), lambda j: (0, 0, 0, j)),
        out_shape=jax.ShapeDtypeStruct((2, n, WIDE, C), BF16),
        cost_estimate=pl.CostEstimate(
            flops=n * 2 * WIDE * C * 18, bytes_accessed=(n + 5) * 2 * WIDE * C * 2, transcendentals=0
        ),
        name=name,
    )(*ins)


def project_kernel(tokens_of, n_smooth, acc_in, where_ref, *refs):
    x_ref = refs[0]
    smooth_refs = refs[1 : 1 + n_smooth]
    rest = refs[1 + n_smooth :]
    time_ref, gain_ref, wq_ref, wk_ref, wv_ref = rest[:5]
    rest = rest[5:]
    if acc_in:
        keep_in, send_in = rest[:2]
        rest = rest[2:]
    q_ref, keep_ref, send_ref, normed_ref, hidden_ref = rest
    step = pl.program_id(0)
    tokens = len(tokens_of) * WIDE
    half = tokens // 2

    @pl.when(step == 0)
    def _():
        for n, (f, row, sources) in enumerate(tokens_of):

            def mix(k, total):
                ds = pl.ds(pl.multiple_of(k * 128, 128), 128)
                t = time_ref[:, ds].astype(F32)
                s = [smooth_refs[i][g, r, :, ds].astype(F32) for i, g, r in sources]
                hidden = x_ref[f, row, :, ds].astype(F32) + (
                    t[0:1] * s[0] + t[1:2] * s[1] + t[2:3] * s[2]
                )
                hidden_ref[:, ds] = hidden
                return total + hidden * hidden

            total = lax.fori_loop(0, C // 128, mix, jnp.zeros((WIDE, 128), F32), unroll=4)
            inverse = lax.rsqrt(jnp.sum(total, axis=1, keepdims=True) * (1.0 / C) + epsilon)

            def scale(k, carry):
                ds = pl.ds(pl.multiple_of(k * 128, 128), 128)
                normed_ref[n * WIDE : (n + 1) * WIDE, ds] = (
                    hidden_ref[:, ds] * inverse * gain_ref[:, ds]
                ).astype(BF16)
                return carry

            lax.fori_loop(0, C // 128, scale, 0, unroll=4)

    normed = normed_ref[...]

    def feature(p):
        return jnp.where(p > 0.0, p + 1.0, jnp.exp(jnp.minimum(p, 0.0))).astype(BF16)

    q_ref[...] = feature(jnp.dot(normed, wq_ref[...], preferred_element_type=F32))
    k = feature(jnp.dot(normed, wk_ref[...], preferred_element_type=F32))
    v = jnp.dot(normed, wv_ref[...], preferred_element_type=F32).astype(BF16)
    mine = where_ref[1] == 0
    for u in range(2):
        ku, vu = k[u * half : (u + 1) * half], v[u * half : (u + 1) * half]
        both = lax.dot_general(vu, ku, (((0,), (0,)), ((), ())), preferred_element_type=F32)
        sums = jnp.sum(ku.astype(F32), axis=0, keepdims=True)
        st = [
            jnp.concatenate(
                [
                    both[h * 128 : (h + 1) * 128, h * 128 : (h + 1) * 128],
                    jnp.broadcast_to(sums[:, h * 128 : (h + 1) * 128], (16, 128)),
                ],
                axis=0,
            )
            for h in range(2)
        ]
        kept = jnp.where(mine, st[0], st[1])
        sent = jnp.where(mine, st[1], st[0])
        if acc_in:
            kept = kept + keep_in[0, u]
            sent = sent + send_in[0, u]
        keep_ref[0, u] = kept.astype(keep_ref.dtype)
        send_ref[0, u] = sent.astype(send_ref.dtype)


def project(where, frames, pair, smooths, tokens_of, time_taps, gain, w_qkv, partial, out_dtype, name):
    tokens = len(tokens_of) * WIDE
    full = lambda a: pl.BlockSpec(a.shape, lambda j, w, n=a.ndim: (0,) * n, pipeline_mode=pl.Buffered(1))
    ins = [frames, *smooths, time_taps, gain, w_qkv, w_qkv, w_qkv]
    specs = [
        pl.BlockSpec((2, ROWS, WIDE, C), lambda j, w: (pair, 0, 0, 0), pipeline_mode=pl.Buffered(1)),
        *[full(s) for s in smooths],
        full(time_taps),
        full(gain),
        pl.BlockSpec((C, 256), lambda j, w: (0, w[0] ^ j)),
        pl.BlockSpec((C, 256), lambda j, w: (0, 4 + (w[0] ^ j))),
        pl.BlockSpec((C, 256), lambda j, w: (0, 8 + (w[0] ^ j))),
    ]
    st_spec = pl.BlockSpec((1, 2, ST, HEAD), lambda j, w: (j, 0, 0, 0))
    if partial is not None:
        ins += list(partial)
        specs += [st_spec, st_spec]
    st_shape = jax.ShapeDtypeStruct((4, 2, ST, HEAD), out_dtype)
    return pl.pallas_call(
        functools.partial(project_kernel, tokens_of, len(smooths), partial is not None),
        grid_spec=pltpu.PrefetchScalarGridSpec(
            num_scalar_prefetch=1,
            grid=(4,),
            in_specs=specs,
            out_specs=[pl.BlockSpec((tokens, 256), lambda j, w: (0, w[0] ^ j)), st_spec, st_spec],
            scratch_shapes=[pltpu.VMEM((tokens, C), BF16), pltpu.VMEM((WIDE, C), F32)],
        ),
        out_shape=[jax.ShapeDtypeStruct((tokens, 1024), BF16), st_shape, st_shape],
        compiler_params=pltpu.CompilerParams(vmem_limit_bytes=56 * 1024 * 1024),
        cost_estimate=pl.CostEstimate(
            flops=tokens * C * 3072 * 2, bytes_accessed=C * 3072 * 2 + tokens * C * 8, transcendentals=0
        ),
        name=name,
    )(where, *ins)


def small(kernel, outs, *ins, name):
    return pl.pallas_call(
        kernel,
        out_shape=[jax.ShapeDtypeStruct(s, d) for s, d in outs],
        cost_estimate=pl.CostEstimate(flops=1000000, bytes_accessed=1000000, transcendentals=0),
        name=name,
    )(*ins)


def sum_core(keep, recv, o0, o1, o2, o3):
    for r, o in enumerate((o0, o1, o2, o3)):
        o[...] = (keep[r].astype(F32) + recv[r].astype(F32)).astype(o.dtype)


def sum_four(a, b, c, d, own, sent):
    total = (a[...].astype(F32) + b[...].astype(F32)) + (c[...].astype(F32) + d[...].astype(F32))
    own[...] = total
    sent[...] = total.astype(BF16)


def sum_early(a, b, c, d, gathered, total_ref):
    total = (a[...] + b[...].astype(F32)) + (c[...].astype(F32) + d[...].astype(F32))
    both = total[0] + total[1]
    gathered[0] = total[0].astype(BF16)
    gathered[1] = both.astype(BF16)
    total_ref[...] = both


def sum_late(a, b, c, d, early, own, group):
    total = (a[...] + b[...].astype(F32)) + (c[...].astype(F32) + d[...].astype(F32))
    own[...] = total
    group[...] = (total[0] + total[1] + early[...]).astype(BF16)


def sum_prefix(own, b1, b2, b3, out):
    before = b1[...].astype(F32) + b2[...].astype(F32) + b3[...].astype(F32)
    first = before + own[0]
    out[0] = first.astype(BF16)
    out[1] = (first + own[1]).astype(BF16)


SLICE = (2, ST, HEAD)


def reduced(keep, send, tag):
    recv = along_core(send)
    o = small(sum_core, [(SLICE, F32)] + [(SLICE, BF16)] * 3, keep, recv, name="core_" + tag)
    r = [along_x(o[i], i) for i in (1, 2, 3)]
    own, sent = small(sum_four, [(SLICE, F32), (SLICE, BF16)], o[0], *r, name="x_" + tag)
    return own, [along_z(sent, i) for i in (1, 2, 3)]


def gathered(a):
    mine = [a] + [along_x(a, r) for r in (1, 2, 3)]
    return mine + [along_core(m) for m in mine]


def attend_kernel(where_ref, q_mid, q_edge, q_last, *refs):
    late, early = refs[:8], refs[8:16]
    w_ref, gain_ref, out_ref, right_ref, mixed_ref = refs[16:]
    f = pl.program_id(0)
    x, c = where_ref[0], where_ref[1]
    for rc in range(2):
        for rx in range(4):
            j = rc * 4 + rx
            h = 2 * (x ^ rx) + (c ^ rc)
            base = late[j][jnp.minimum(f, 1)].astype(F32)
            more = early[j][jnp.maximum(f - 2, 0)].astype(F32)
            st = base + jnp.where(f >= 2, more, 0.0)
            right_ref[h, 0:128, :] = st[0:128].astype(BF16)
            right_ref[h, 128:256, :] = jnp.broadcast_to(st[128:129], (128, 128)).astype(BF16)

    def heads(rows, q):
        for h in range(HEADS):
            both = lax.dot_general(
                q(h), right_ref[h], (((1,), (1,)), ((), ())), preferred_element_type=F32
            )
            mixed_ref[rows, h * 128 : (h + 1) * 128] = (both[:, :128] / both[:, 128:]).astype(BF16)

    @pl.when(f < 2)
    def _():
        def q(h):
            cols = slice(h * 128, (h + 1) * 128)
            mid = q_mid[:, cols]
            edge = q_edge[:, cols]
            return jnp.concatenate([edge[:WIDE], mid, edge[WIDE:]], axis=0)

        heads(slice(None), q)

    @pl.when(f >= 2)
    def _():
        heads(slice(None), lambda h: q_last[:, h * 128 : (h + 1) * 128])

    branch = jnp.dot(mixed_ref[...], w_ref[...], preferred_element_type=F32)
    inverse = lax.rsqrt(jnp.mean(branch * branch, axis=1, keepdims=True) + epsilon)
    out_ref[...] = (branch * inverse * gain_ref[...]).astype(BF16).reshape(out_ref.shape)


def attend(where, q_mid, q_edge, q_last, late, early, w_out, out_gain):
    full = lambda a: pl.BlockSpec(a.shape, lambda j, w, n=a.ndim: (0,) * n, pipeline_mode=pl.Buffered(1))
    ins = [q_mid, q_edge, q_last, *late, *early, w_out, out_gain]
    specs = [
        pl.BlockSpec((128, 1024), lambda j, w: (jnp.minimum(j, 1), 0)),
        pl.BlockSpec((128, 1024), lambda j, w: (jnp.minimum(j, 1), 0)),
        pl.BlockSpec((256, 1024), lambda j, w: (jnp.maximum(j - 2, 0), 0)),
        *[full(a) for a in (*late, *early, w_out, out_gain)],
    ]
    return pl.pallas_call(
        attend_kernel,
        grid_spec=pltpu.PrefetchScalarGridSpec(
            num_scalar_prefetch=1,
            grid=(4,),
            in_specs=specs,
            out_specs=pl.BlockSpec((1, ROWS, WIDE, C), lambda j, w: (j, 0, 0, 0)),
            scratch_shapes=[pltpu.VMEM((HEADS, 256, 128), BF16), pltpu.VMEM((256, 1024), BF16)],
        ),
        out_shape=jax.ShapeDtypeStruct((4, ROWS, WIDE, C), BF16),
        compiler_params=pltpu.CompilerParams(vmem_limit_bytes=56 * 1024 * 1024),
        cost_estimate=pl.CostEstimate(flops=1024 * 1024 * 2048 * 2, bytes_accessed=16 << 20, transcendentals=0),
        name="attend",
    )(where, *ins)


def local(frames, spatial_taps, time_taps, norm_gain, w_qkv, w_out, out_gain):
    place = lax.axis_index("space").astype(jnp.int32)
    where = jnp.stack([(place // 2) % 4, place % 2])
    gain = norm_gain.reshape(1, C)
    ogain = out_gain.reshape(1, C)

    def halo(pair):
        up = [(i, i + 1) for i in range(31)]
        down = [(i + 1, i) for i in range(31)]
        part = frames[2 * pair : 2 * pair + 2]
        return (
            lax.ppermute(part[:, ROWS - 1 :], "space", up),
            lax.ppermute(part[:, :1], "space", down),
        )

    halo_last = halo(1)
    mid = conv(frames, 1, (1, 2), None, spatial_taps, "filter_mid")
    mid_before = along_tm(mid, 1)
    edge = conv(frames, 1, (0, 3), halo_last, spatial_taps, "filter_edge")
    edge_before = along_tm(edge, 1)
    halo_first = halo(0)
    first = conv(frames, 0, (0, 1, 2, 3), halo_first, spatial_taps, "filter_first")

    shared = (time_taps, gain, w_qkv)

    def last_row(f, r):
        return (1, f, r - 1) if r in (1, 2) else (2, f, 0 if r == 0 else 1)

    tokens = []
    for f in range(2):
        for r in range(ROWS):
            now = last_row(f, r)
            one = (0, 1, r) if f == 0 else last_row(0, r)
            two = (0, f, r)
            tokens.append((f, r, (now, one, two)))
    q_last, keep, send = project(
        where, frames, 1, [first, mid, edge], tokens, *shared, None, BF16, "project_last"
    )
    own, z = reduced(keep, send, "early")
    early, early_total = small(
        sum_early, [(SLICE, BF16), (SLICE[1:], F32)], own, *z, name="z_early"
    )
    early_all = gathered(early)

    def first_tokens(rows):
        tokens = []
        for f in range(2):
            for n, r in enumerate(rows):
                now = (0, f, r)
                one = (1, 1, n) if f == 0 else (0, 0, r)
                two = (1, f, n)
                tokens.append((f, r, (now, one, two)))
        return tokens

    q_mid, keep, send = project(
        where, frames, 0, [first, mid_before], first_tokens((1, 2)), *shared, None, F32, "project_mid"
    )
    q_edge, keep, send = project(
        where, frames, 0, [first, edge_before], first_tokens((0, 3)), *shared, (keep, send), BF16, "project_edge"
    )
    own, z = reduced(keep, send, "late")
    own, group = small(
        sum_late, [(SLICE, F32), (SLICE[1:], BF16)], own, *z, early_total, name="z_late"
    )
    before = [along_tm(group, by) for by in (1, 2, 3)]
    (prefix,) = small(sum_prefix, [(SLICE, BF16)], own, *before, name="prefix")
    late_all = gathered(prefix)
    return attend(where, q_mid, q_edge, q_last, late_all, early_all, w_out, ogain)


def solution(mesh):
    return jax.shard_map(
        local,
        mesh=mesh,
        in_specs=(P("tm", "space", None, None), P(), P(), P(), P(), P(), P()),
        out_specs=P("tm", "space", None, None),
        check_vma=False,
    )
```

```python
import functools

import jax
import jax.numpy as jnp
from jax import lax
from jax.experimental import pallas as pl
from jax.experimental.pallas import tpu as pltpu
from jax.sharding import PartitionSpec as P

HEADS = 8
HEAD = 128
C = 2048
WIDE = 64
ROWS = 4
ST = 144
F32 = jnp.float32
BF16 = jnp.bfloat16
epsilon = 1e-06


def space_pairs(move):
    pairs = []
    for s in range(32):
        z, x, c = s // 8, (s // 2) % 4, s % 2
        z2, x2, c2 = move(z, x, c)
        pairs.append((s, (z2 * 4 + x2) * 2 + c2))
    return pairs


def along_core(a):
    return lax.ppermute(a, "space", space_pairs(lambda z, x, c: (z, x, 1 - c)))


def along_x(a, r):
    return lax.ppermute(a, "space", space_pairs(lambda z, x, c: (z, x ^ r, c)))


def along_z(a, r):
    return lax.ppermute(a, "space", space_pairs(lambda z, x, c: (z ^ r, x, c)))


def along_tm(a, by):
    return lax.ppermute(a, "tm", [(i, i + by) for i in range(4 - by)])


VM = pl.BlockSpec(memory_space=pltpu.VMEM)
SM = pl.BlockSpec(memory_space=pltpu.SMEM)
MIB = 1024 * 1024


def call(kernel, outs, ins, after, name, limit, flops, nbytes, scratch=(), smem=0):
    def body(*refs):
        kernel(*refs[: len(ins)], *refs[len(ins) + len(after) :])

    return pl.pallas_call(
        body,
        in_specs=[SM] * smem + [VM] * (len(ins) - smem + len(after)),
        out_specs=[VM] * len(outs),
        out_shape=[jax.ShapeDtypeStruct(s, d) for s, d in outs],
        scratch_shapes=list(scratch),
        compiler_params=pltpu.CompilerParams(vmem_limit_bytes=limit * MIB),
        cost_estimate=pl.CostEstimate(flops=flops, bytes_accessed=nbytes, transcendentals=0),
        name=name,
    )(*ins, *after)


def conv_kernel(pair, rows, x_ref, *refs):
    if len(refs) == 4:
        up_ref, down_ref, taps_ref, out_ref = refs
    else:
        taps_ref, out_ref = refs

    def body(k, carry):
        ds = pl.ds(pl.multiple_of(k * 128, 128), 128)
        taps = taps_ref[:, ds].astype(F32)
        w = [taps[i : i + 1] for i in range(9)]
        place = lax.broadcasted_iota(jnp.int32, (WIDE, 128), 0)
        first, last = place == 0, place == WIDE - 1
        for f in range(2):
            held = {}

            def get(i):
                if i not in held:
                    if i < 0:
                        held[i] = up_ref[2 * pair + f, 0, :, ds].astype(F32)
                    elif i >= ROWS:
                        held[i] = down_ref[2 * pair + f, 0, :, ds].astype(F32)
                    else:
                        held[i] = x_ref[2 * pair + f, i, :, ds].astype(F32)
                return held[i]

            for n, i in enumerate(rows):
                a, m, b = get(i - 1), get(i), get(i + 1)
                left = w[0] * a + w[3] * m + w[6] * b
                mid = w[1] * a + w[4] * m + w[7] * b
                right = w[2] * a + w[5] * m + w[8] * b
                left = jnp.where(first, 0.0, pltpu.roll(left, 1, 0))
                right = jnp.where(last, 0.0, pltpu.roll(right, WIDE - 1, 0))
                out_ref[f, n, :, ds] = (left + mid + right).astype(BF16)
        return carry

    lax.fori_loop(0, C // 128, body, 0)


PAIR = (2, 2, WIDE, C)


def conv(frames, pair, rows, halo, taps, after, name):
    ins = [frames, *halo, taps]
    (out,) = call(
        functools.partial(conv_kernel, pair, rows), [(PAIR, BF16)], ins, after, name, 8,
        256 * C * 18, 256 * C * 2,
    )
    return out


def borders(frames, after):
    def kernel(x_ref, token_ref, top_ref, bottom_ref, sems):
        one = pltpu.make_async_copy(x_ref.at[:, 0:1], top_ref, sems.at[0])
        two = pltpu.make_async_copy(x_ref.at[:, ROWS - 1 : ROWS], bottom_ref, sems.at[1])
        one.start()
        two.start()
        one.wait()
        two.wait()

    shape = jax.ShapeDtypeStruct((4, 1, WIDE, C), BF16)
    return pl.pallas_call(
        kernel,
        in_specs=[VM, VM],
        out_specs=[VM, VM],
        out_shape=[shape, shape],
        scratch_shapes=[pltpu.SemaphoreType.DMA((2,))],
        compiler_params=pltpu.CompilerParams(vmem_limit_bytes=4 * MIB),
        cost_estimate=pl.CostEstimate(flops=0, bytes_accessed=4 * MIB, transcendentals=0),
        name="borders",
    )(frames, after)


def project_kernel(pair, rows, acc_in, where_ref, x_ref, now_ref, before_ref, time_ref, gain_ref, w_ref, *rest):
    if acc_in:
        keep_in, send_in = rest[:2]
        rest = rest[2:]
    q_ref, keep_ref, send_ref, normed_ref, hidden_ref = rest
    for f in range(2):
        for n in range(2):
            if f == 0:
                sources = ((now_ref, 0), (before_ref, 1), (before_ref, 0))
            else:
                sources = ((now_ref, 1), (now_ref, 0), (before_ref, 1))
            base = (2 * f + n) * WIDE

            def mix(k, total):
                ds = pl.ds(pl.multiple_of(k * 128, 128), 128)
                t = time_ref[:, ds].astype(F32)
                s = [ref[g, n, :, ds].astype(F32) for ref, g in sources]
                hidden = x_ref[2 * pair + f, rows[n], :, ds].astype(F32) + (
                    t[0:1] * s[0] + t[1:2] * s[1] + t[2:3] * s[2]
                )
                hidden_ref[:, ds] = hidden
                return total + hidden * hidden

            total = lax.fori_loop(0, C // 128, mix, jnp.zeros((WIDE, 128), F32), unroll=4)
            inverse = lax.rsqrt(jnp.sum(total, axis=1, keepdims=True) * (1.0 / C) + epsilon)

            def scale(k, carry):
                ds = pl.ds(pl.multiple_of(k * 128, 128), 128)
                normed_ref[base : base + WIDE, ds] = (
                    hidden_ref[:, ds] * inverse * gain_ref[:, ds]
                ).astype(BF16)
                return carry

            lax.fori_loop(0, C // 128, scale, 0, unroll=4)

    def feature(p):
        return jnp.where(p > 0.0, p + 1.0, jnp.exp(jnp.minimum(p, 0.0))).astype(BF16)

    x, mine = where_ref[0], where_ref[1] == 0
    for rx in range(4):
        at = pl.multiple_of((x ^ rx) * 256, 256)
        normed = normed_ref[...]
        q = jnp.dot(normed, w_ref[:, pl.ds(at, 256)], preferred_element_type=F32)
        q_ref[:, pl.ds(at, 256)] = feature(q)
        k = feature(jnp.dot(normed, w_ref[:, pl.ds(at + 1024, 256)], preferred_element_type=F32))
        v = jnp.dot(normed, w_ref[:, pl.ds(at + 2048, 256)], preferred_element_type=F32).astype(BF16)
        for u in range(2):
            ku, vu = k[u * 128 : (u + 1) * 128], v[u * 128 : (u + 1) * 128]
            both = lax.dot_general(vu, ku, (((0,), (0,)), ((), ())), preferred_element_type=F32)
            sums = jnp.sum(ku.astype(F32), axis=0, keepdims=True)
            st = [
                jnp.concatenate(
                    [
                        both[h * 128 : (h + 1) * 128, h * 128 : (h + 1) * 128],
                        jnp.broadcast_to(sums[:, h * 128 : (h + 1) * 128], (16, 128)),
                    ],
                    axis=0,
                )
                for h in range(2)
            ]
            kept = jnp.where(mine, st[0], st[1])
            sent = jnp.where(mine, st[1], st[0])
            if acc_in:
                kept = kept + keep_in[rx, u]
                sent = sent + send_in[rx, u]
            keep_ref[rx, u] = kept.astype(keep_ref.dtype)
            send_ref[rx, u] = sent.astype(send_ref.dtype)


def project(where, frames, pair, rows, now, before, time_taps, gain, w_qkv, partial, after, name):
    dtype = F32 if partial is None else BF16
    shape = (4, 2, ST, HEAD)
    ins = [where, frames, now, before, time_taps, gain, w_qkv, *(partial or ())]
    return call(
        functools.partial(project_kernel, pair, rows, partial is not None),
        [((256, 1024), BF16), (shape, dtype), (shape, dtype)],
        ins, after, name, 16, 256 * C * 3072 * 2, 256 * C * 8,
        scratch=[pltpu.VMEM((256, C), BF16), pltpu.VMEM((WIDE, C), F32)], smem=1,
    )


def small(kernel, outs, *ins, name, after=()):
    return call(kernel, outs, ins, after, name, 4, 1000000, 1000000)


def sum_core(keep, recv, o0, o1, o2, o3):
    for r, o in enumerate((o0, o1, o2, o3)):
        o[...] = (keep[r].astype(F32) + recv[r].astype(F32)).astype(o.dtype)


def sum_four(a, b, c, d, own, sent):
    total = (a[...].astype(F32) + b[...].astype(F32)) + (c[...].astype(F32) + d[...].astype(F32))
    own[...] = total
    sent[...] = total.astype(BF16)


def sum_early(a, b, c, d, gathered, total_ref):
    total = (a[...] + b[...].astype(F32)) + (c[...].astype(F32) + d[...].astype(F32))
    both = total[0] + total[1]
    gathered[0] = total[0].astype(BF16)
    gathered[1] = both.astype(BF16)
    total_ref[...] = both


def sum_late(a, b, c, d, early, own, group):
    total = (a[...] + b[...].astype(F32)) + (c[...].astype(F32) + d[...].astype(F32))
    own[...] = total
    group[...] = (total[0] + total[1] + early[...]).astype(BF16)


def sum_prefix(own, b1, b2, b3, out):
    before = b1[...].astype(F32) + b2[...].astype(F32) + b3[...].astype(F32)
    first = before + own[0]
    out[0] = first.astype(BF16)
    out[1] = (first + own[1]).astype(BF16)


SLICE = (2, ST, HEAD)


def reduced(keep, send, tag, after=()):
    recv = along_core(send)
    o = small(sum_core, [(SLICE, F32)] + [(SLICE, BF16)] * 3, keep, recv, name="core_" + tag, after=after)
    r = [along_x(o[i], i) for i in (1, 2, 3)]
    own, sent = small(sum_four, [(SLICE, F32), (SLICE, BF16)], o[0], *r, name="x_" + tag)
    return own, [along_z(sent, i) for i in (1, 2, 3)]


def gathered(a):
    mine = [a] + [along_x(a, r) for r in (1, 2, 3)]
    return mine + [along_core(m) for m in mine]


def attend_kernel(where_ref, q_first_mid, q_first_edge, q_last_mid, q_last_edge, *refs):
    late, early = refs[:8], refs[8:16]
    w_ref, gain_ref, out_ref, right_ref, mixed_ref = refs[16:]
    f = pl.program_id(0)
    x, c = where_ref[0], where_ref[1]
    for rc in range(2):
        for rx in range(4):
            j = rc * 4 + rx
            h = 2 * (x ^ rx) + (c ^ rc)
            base = late[j][jnp.minimum(f, 1)].astype(F32)
            more = early[j][jnp.maximum(f - 2, 0)].astype(F32)
            st = base + jnp.where(f >= 2, more, 0.0)
            right_ref[h, 0:128, :] = st[0:128].astype(BF16)
            right_ref[h, 128:256, :] = jnp.broadcast_to(st[128:129], (128, 128)).astype(BF16)

    def heads(mid_ref, edge_ref, g):
        for h in range(HEADS):
            cols = slice(h * 128, (h + 1) * 128)
            mid = mid_ref[g * 128 : (g + 1) * 128, cols]
            edge = edge_ref[g * 128 : (g + 1) * 128, cols]
            q = jnp.concatenate([edge[:WIDE], mid, edge[WIDE:]], axis=0)
            both = lax.dot_general(
                q, right_ref[h], (((1,), (1,)), ((), ())), preferred_element_type=F32
            )
            mixed_ref[:, cols] = (both[:, :128] / both[:, 128:]).astype(BF16)

    for i, (mid_ref, edge_ref) in enumerate(((q_first_mid, q_first_edge), (q_last_mid, q_last_edge))):
        for g in range(2):

            @pl.when(f == 2 * i + g)
            def _(mid_ref=mid_ref, edge_ref=edge_ref, g=g):
                heads(mid_ref, edge_ref, g)

    branch = jnp.dot(mixed_ref[...], w_ref[...], preferred_element_type=F32)
    inverse = lax.rsqrt(jnp.mean(branch * branch, axis=1, keepdims=True) + epsilon)
    out_ref[...] = (branch * inverse * gain_ref[...]).astype(BF16).reshape(out_ref.shape)


def attend(where, qs, late, early, w_out, out_gain):
    ins = [where, *qs, *late, *early, w_out, out_gain]
    return pl.pallas_call(
        attend_kernel,
        grid=(4,),
        in_specs=[SM] + [VM] * (len(ins) - 1),
        out_specs=pl.BlockSpec((1, ROWS, WIDE, C), lambda j: (j, 0, 0, 0)),
        scratch_shapes=[pltpu.VMEM((HEADS, 256, 128), BF16), pltpu.VMEM((256, 1024), BF16)],
        out_shape=jax.ShapeDtypeStruct((4, ROWS, WIDE, C), BF16),
        compiler_params=pltpu.CompilerParams(vmem_limit_bytes=20 * MIB),
        cost_estimate=pl.CostEstimate(flops=1024 * 1024 * 2048 * 2, bytes_accessed=16 << 20, transcendentals=0),
        name="attend",
    )(*ins)


def local(frames, spatial_taps, time_taps, norm_gain, w_qkv, w_out, out_gain):
    place = lax.axis_index("space").astype(jnp.int32)
    where = jnp.stack([(place // 2) % 4, place % 2])
    gain = norm_gain.reshape(1, C)
    ogain = out_gain.reshape(1, C)
    shared = (time_taps, gain, w_qkv)
    mid, edge = (1, 2), (0, 3)

    mid_last = conv(frames, 1, mid, (), spatial_taps, (), "filter_mid_last")
    mid_before = along_tm(mid_last, 1)
    top, bottom = borders(frames, mid_last)
    halo = (
        lax.ppermute(bottom, "space", [(i, i + 1) for i in range(31)]),
        lax.ppermute(top, "space", [(i + 1, i) for i in range(31)]),
    )
    mid_first = conv(frames, 0, mid, (), spatial_taps, (top,), "filter_mid_first")
    q_lm, *partial = project(where, frames, 1, mid, mid_last, mid_first, *shared, None, (), "last_mid")
    edge_last = conv(frames, 1, edge, halo, spatial_taps, (q_lm,), "filter_edge_last")
    edge_before = along_tm(edge_last, 1)
    edge_first = conv(frames, 0, edge, halo, spatial_taps, (edge_last,), "filter_edge_first")
    q_le, keep, send = project(
        where, frames, 1, edge, edge_last, edge_first, *shared, partial, (), "last_edge"
    )
    q_fm, *partial = project(
        where, frames, 0, mid, mid_first, mid_before, *shared, None, (q_le,), "first_mid"
    )
    own, z = reduced(keep, send, "early", (q_fm,))
    early, early_total = small(
        sum_early, [(SLICE, BF16), (SLICE[1:], F32)], own, *z, name="z_early"
    )
    early_all = gathered(early)
    q_fe, keep, send = project(
        where, frames, 0, edge, edge_first, edge_before, *shared, partial, tuple(early_all[1:4]), "first_edge"
    )
    own, z = reduced(keep, send, "late")
    own, group = small(
        sum_late, [(SLICE, F32), (SLICE[1:], BF16)], own, *z, early_total, name="z_late"
    )
    before = [along_tm(group, by) for by in (1, 2, 3)]
    (prefix,) = small(sum_prefix, [(SLICE, BF16)], own, *before, name="prefix")
    late_all = gathered(prefix)
    return attend(where, (q_fm, q_fe, q_lm, q_le), late_all, early_all, w_out, ogain)


def solution(mesh):
    return jax.shard_map(
        local,
        mesh=mesh,
        in_specs=(P("tm", "space", None, None), P(), P(), P(), P(), P(), P()),
        out_specs=P("tm", "space", None, None),
        check_vma=False,
    )
```
